512 devices in a mesh: rep: 8 (over y, core), ep: 64 (over x, z).
Axes of the slice: x: 4, y: 4, z: 16, core: 2. Of those that a mesh axis runs over, the one named last changes fastest.
Arguments:
- hidden_state: bfloat16 [1024, 4096], P(('ep', 'rep')), may hold values from -6 to 6
- norm_gain: float32 [4096], replicated, may hold values from 0.5 to 1.5
- expert_ids: int32 [1024, 8], P('ep'), may hold values from 0 to 63, as said below
- gate_logits: float32 [1024, 8], P('ep'), may hold values from -4 to 4
- gate_weight: bfloat16 [64, 4096, 1024], P('ep', None, 'rep'), may hold values from -0.09375 to 0.09375
- up_weight: bfloat16 [64, 4096, 1024], P('ep', None, 'rep'), may hold values from -0.09375 to 0.09375
- down_weight: bfloat16 [64, 1024, 4096], P('ep', 'rep'), may hold values from -0.1875 to 0.1875
Outputs:
- moe_out: bfloat16 [1024, 4096], P(('ep', 'rep'))
The draws below stay inside these ranges and needn't reach their ends.
Inputs may be any that keep to these rules, and one draw needn't show every extreme that they name: `expert_ids`: in each aligned block of 16 rows, each row names 8 different experts; two experts, the same in every block, are each named by exactly 9 rows of the block; every other expert by at most 2 rows of a block, a bound reached in every block.
All inputs are finite; a program needn't handle non-finite values.
Results may differ from the reference program's by a relative error of at most 0.0065.
Values may be sent and summed in bfloat16 or wider, within the bound.
A program may use at most 128 MiB of HBM per device.

```python
import jax
import jax.numpy as jnp
from jax import lax

D = 4096
FF = 1024
TOP = 8
EXPERTS = 64
COL = 16
ROWS = 1024
HOT = 9
COLD_CAP = 2
N_EP = 64


def block_ranks(key, block_count):
    scores = jax.random.randint(key, (block_count, COL), 0, 1048576) * COL + jnp.arange(COL, dtype=jnp.int32)[None, :]
    return jnp.argsort(jnp.argsort(scores, axis=1), axis=1).astype(jnp.int32)


def draw_expert_ids(key, part):
    block_count = ROWS // COL
    cold_count = EXPERTS - 2
    key_order, key_first, key_second, key_offset, key_shuffle = jax.random.split(key, 5)
    expert_order = jax.random.permutation(key_order, EXPERTS).astype(jnp.int32)
    first_hot = expert_order[0]
    second_hot = expert_order[1]
    cold_list = expert_order[2:]
    first_flag = (block_ranks(key_first, block_count) < HOT).astype(jnp.int32)
    second_flag = (block_ranks(key_second, block_count) < HOT).astype(jnp.int32)
    cold_slots = TOP - first_flag - second_flag
    cold_start = jnp.cumsum(cold_slots, axis=1) - cold_slots
    offset = jax.random.randint(key_offset, (block_count, 1, 1), 0, cold_count)
    slot_index = jnp.arange(TOP, dtype=jnp.int32)[None, None, :]
    hot_slots = (first_flag + second_flag)[:, :, None]
    cold_index = (cold_start[:, :, None] + slot_index - hot_slots + offset) % cold_count
    chosen = jnp.where(slot_index < first_flag[:, :, None], first_hot, jnp.where(slot_index < hot_slots, second_hot, cold_list[cold_index]))
    shuffle_scores = jax.random.randint(key_shuffle, (block_count, COL, TOP), 0, 1048576) * TOP + slot_index
    shuffle_order = jnp.argsort(shuffle_scores, axis=2)
    chosen = jnp.take_along_axis(chosen, shuffle_order, axis=2)
    return chosen.reshape(ROWS, TOP).astype(jnp.int32)


def shard_levels(own_key, shape, cuts, smallest, largest):
    def one(axis_at, blocks):
        heights = jax.random.uniform(jax.random.fold_in(jax.random.fold_in(own_key, 6), axis_at), (blocks,), jnp.float32, smallest / len(cuts), largest / len(cuts))
        return jnp.repeat(jnp.exp(heights), shape[axis_at] // blocks).reshape((-1,) + (1,) * (len(shape) - axis_at - 1))

    loudness = one(*cuts[0])
    for cut in cuts[1:]:
        loudness = loudness * one(*cut)
    return loudness


def bell_draw(own_key, extent, spread, reach, shards=(), kind=jnp.bfloat16):
    values = spread * jax.random.normal(own_key, extent, jnp.float32)
    if shards:
        values = values * shard_levels(own_key, extent, shards, -0.22, 0.18)
    return jnp.clip(values, -reach, reach).astype(kind)


def setup_inputs(seed: int = 0) -> dict:
    keys = jax.random.split(jax.random.key(seed), 8)
    hidden_state = bell_draw(keys[0], (ROWS, D), 1.0, 6.0, ((0, 512),))
    norm_gain = jnp.clip(1.0 + 0.1 * jax.random.normal(keys[1], (D,), jnp.float32), 0.5, 1.5)
    expert_ids = draw_expert_ids(jax.random.fold_in(keys[7], 71), 0)
    gate_logits = bell_draw(keys[3], (ROWS, TOP), 1.0, 4.0, ((0, 64),), jnp.float32)
    gate_weight = bell_draw(keys[4], (EXPERTS, D, FF), D ** -0.5, 0.09375, ((0, 64), (2, 8)))
    up_weight = bell_draw(keys[5], (EXPERTS, D, FF), D ** -0.5, 0.09375, ((0, 64), (2, 8)))
    down_weight = bell_draw(keys[6], (EXPERTS, FF, D), FF ** -0.5, 0.1875, ((0, 64), (1, 8)))
    return dict(hidden_state=hidden_state, norm_gain=norm_gain, expert_ids=expert_ids, gate_logits=gate_logits, gate_weight=gate_weight, up_weight=up_weight, down_weight=down_weight)


epsilon = 1e-06

def normalize(hidden_state, norm_gain):
    values = hidden_state.astype(jnp.float32)
    inverse_rms = lax.rsqrt(lax.optimization_barrier(jnp.mean(values * values, axis=-1, keepdims=True)) + epsilon)
    return (values * inverse_rms * norm_gain.astype(jnp.float32)).astype(jnp.bfloat16)

def expert_apply(row_block, gate_matrix, up_matrix, down_matrix):
    gate_part = jnp.dot(row_block, gate_matrix, preferred_element_type=jnp.float32)
    up_part = jnp.dot(row_block, up_matrix, preferred_element_type=jnp.float32)
    activation = (jax.nn.silu(gate_part) * up_part).astype(jnp.bfloat16)
    return jnp.dot(activation, down_matrix, preferred_element_type=jnp.float32)

def reference(hidden_state, norm_gain, expert_ids, gate_logits, gate_weight, up_weight, down_weight):
    normed = normalize(hidden_state, norm_gain)
    exp_logits = jnp.exp(gate_logits.astype(jnp.float32))
    gate_probs = exp_logits / lax.optimization_barrier(jnp.sum(exp_logits, axis=1, keepdims=True))
    labels = jnp.arange(EXPERTS, dtype=jnp.int32)
    counts = lax.optimization_barrier(jnp.sum((expert_ids[:, :, None] == labels).astype(jnp.int32), axis=(0, 1)))
    is_hot = (counts > COLD_CAP * N_EP).astype(jnp.int32)
    first_hot = jnp.argmax(is_hot).astype(jnp.int32)
    second_hot = (EXPERTS - 1 - jnp.argmax(is_hot[::-1])).astype(jnp.int32)

    def accumulate(running, expert_index, gate_matrix, up_matrix, down_matrix, capacity, keep_scale):
        chosen = expert_ids == expert_index
        member = jnp.any(chosen, axis=1).astype(jnp.int32)
        weight = lax.optimization_barrier(jnp.sum(jnp.where(chosen, gate_probs, jnp.float32(0.0)), axis=1)) * keep_scale
        row_order = jnp.argsort(1 - member, stable=True)[:capacity].astype(jnp.int32)
        picked = normed[row_order]
        result = expert_apply(picked, gate_matrix, up_matrix, down_matrix)
        return running.at[row_order].add(result * weight[row_order][:, None])

    def cold_step(running, stacked):
        gate_matrix, up_matrix, down_matrix, expert_index = stacked
        keep_scale = jnp.float32(1.0) - is_hot[expert_index].astype(jnp.float32)
        return (accumulate(running, expert_index, gate_matrix, up_matrix, down_matrix, COLD_CAP * N_EP, keep_scale), None)
    running = jnp.zeros((normed.shape[0], normed.shape[1]), jnp.float32)
    running, unused = lax.scan(cold_step, running, (gate_weight, up_weight, down_weight, labels))
    for hot_index in (first_hot, second_hot):
        running = accumulate(running, hot_index, gate_weight[hot_index], up_weight[hot_index], down_weight[hot_index], HOT * N_EP, jnp.float32(1.0))
    return running.astype(jnp.bfloat16)
```

```python
import functools

import jax
import jax.numpy as jnp
from jax import lax
from jax.experimental import pallas as pl
from jax.experimental.pallas import tpu as pltpu
from jax.sharding import PartitionSpec as P

epsilon = 1e-06
MESH = pl.DeviceIdType.MESH
Y, C, X, Z = 4, 2, 4, 16
REP = Y * C
COL = 16
TOP = 8
ROWS = X * Z * COL
XROWS = Z * COL
D = 4096
SLICE = D // REP
HALF = SLICE // 2
HID = 128


def kernel(
    hid, gain, tab, gw, uw, dw, out,
    SA, SB, BF, R, T, W, ACC, HF, DT, YF, PB, XR, XS, ZS, ZP, ZR, FA, FB,
    lsem, as_, ar, ds_, dr, zs, zr, ts_, tr, xs, xr, ys, yr, ss, sr,
    txs, txr, hs, hr, hss, hsr, rs, rr, zzs, zzr, fs, fr,
):
    rep = lax.axis_index("rep")
    ep = lax.axis_index("ep")
    y, c = rep // C, lax.rem(rep, C)
    x, z = ep // Z, lax.rem(ep, Z)

    def wrap(v, n):
        return lax.rem(v + n, n)

    def at_rep(r):
        return {"rep": r, "ep": ep}

    def at_ep(e):
        return {"rep": rep, "ep": e}

    xl, xri, xo = wrap(x - 1, X), wrap(x + 1, X), wrap(x + 2, X)
    yl, yri, yo = wrap(y - 1, Y), wrap(y + 1, Y), wrap(y + 2, Y)
    dev_xl, dev_xr = at_ep(xl * Z + z), at_ep(xri * Z + z)
    dev_yl, dev_yr = at_rep(yl * C + c), at_rep(yri * C + c)
    dev_sib = at_rep(y * C + 1 - c)
    zdev = [at_ep(x * Z + lax.rem(z + d, Z)) for d in range(1, Z)]
    rdev = [lax.rem(rep + d, REP) for d in range(1, REP)]

    pending = []

    def send(src, dst, ssem, rsem, dev):
        copy = pltpu.make_async_remote_copy(
            src_ref=src, dst_ref=dst, send_sem=ssem, recv_sem=rsem, device_id=dev, device_id_type=MESH
        )
        copy.start()
        pending.append(copy)
        return copy

    loads = [
        pltpu.make_async_copy(gw.at[0], W.at[:, 0:HID], lsem.at[0]),
        pltpu.make_async_copy(uw.at[0], W.at[:, HID:2 * HID], lsem.at[1]),
    ]
    for load in loads:
        load.start()

    barrier = pltpu.get_barrier_semaphore()
    partners = [at_rep(r) for r in rdev] + [dev_xl, dev_xr] + zdev
    for dev in partners:
        pl.semaphore_signal(barrier, inc=1, device_id=dev, device_id_type=MESH)

    values = hid[...].astype(jnp.float32)
    inverse_rms = lax.rsqrt(jnp.mean(values * values, axis=-1, keepdims=True) + epsilon)
    normed = (values * inverse_rms * gain[...]).astype(jnp.bfloat16)
    for r in range(REP):
        SA[r] = normed[:, r * SLICE:(r + 1) * SLICE]
    row0 = pl.multiple_of(ep * COL, COL)
    xrow0 = pl.multiple_of(x * XROWS, XROWS)
    T[pl.ds(row0, COL), :] = tab[...]
    pl.semaphore_wait(barrier, len(partners))

    first = [
        send(SA.at[r], SB.at[rep], as_.at[i], ar.at[i], at_rep(r)) for i, r in enumerate(rdev)
    ]
    tabs = [
        send(T.at[pl.ds(row0, COL)], T.at[pl.ds(row0, COL)], ts_.at[i], tr.at[i], dev)
        for i, dev in enumerate(zdev)
    ]
    SB[rep] = SA[rep]
    for copy in first:
        copy.wait_recv()
    for r in range(REP):
        BF[2 * r:2 * r + 2, :] = SB[r].astype(jnp.float32)
    block = BF[...].astype(jnp.bfloat16)
    R[y, c, 0, pl.ds(row0, COL), :] = block[:, :HALF]
    R[y, c, 1, pl.ds(row0, COL), :] = block[:, HALF:]
    mine = R.at[y, c, :, pl.ds(row0, COL), :]
    along_z = [send(mine, mine, zs.at[i], zr.at[i], dev) for i, dev in enumerate(zdev)]

    downs = [
        send(
            dw.at[0, :, pl.ds(pl.multiple_of(r * SLICE, SLICE), SLICE)],
            DT.at[rep], ds_.at[i], dr.at[i], at_rep(r),
        )
        for i, r in enumerate(rdev)
    ]
    own_down = pltpu.make_async_copy(
        dw.at[0, :, pl.ds(pl.multiple_of(rep * SLICE, SLICE), SLICE)], DT.at[rep], lsem.at[2]
    )
    own_down.start()
    ACC[...] = jnp.zeros_like(ACC)
    for load in loads:
        load.wait()

    class Ring:
        def __init__(self, view, me, n, left, right, ssem, rsem, base):
            self.view, self.me, self.left, self.right = view, me, left, right
            self.lo, self.hi = wrap(me - 1, n), wrap(me + 1, n)
            self.ssem, self.rsem, self.base = ssem, rsem, base

        def put(self, who, half, dev, k):
            k += self.base
            ref = self.view(who, half)
            return send(ref, ref, self.ssem.at[k], self.rsem.at[k], dev)

        def first(self):
            self.ra = self.put(self.me, 0, self.right, 0)
            self.lb = self.put(self.me, 1, self.left, 1)
            self.rb = self.put(self.me, 1, self.right, 2)
            self.la = self.put(self.me, 0, self.left, 3)

        def relay(self):
            self.ra.wait_recv()
            self.oa = self.put(self.lo, 0, self.right, 4)
            self.lb.wait_recv()
            self.ob = self.put(self.hi, 1, self.left, 5)

        def low(self):
            self.rb.wait_recv()

        def high(self):
            self.la.wait_recv()

        def far(self):
            self.oa.wait_recv()
            self.ob.wait_recv()

    def rows(start, size):
        return pl.ds(pl.multiple_of(start, 16), size)

    ring_t = Ring(
        lambda s, h: T.at[rows(s * XROWS + h * 128, 128), :], x, X, dev_xl, dev_xr, txs, txr, 0
    )
    x1 = Ring(
        lambda s, h: R.at[y, c, 0, rows(s * XROWS + h * 128, 128), :], x, X, dev_xl, dev_xr, xs, xr, 0
    )
    y1 = Ring(
        lambda s, h: R.at[s, c, 1, rows(x * XROWS + h * 128, 128), :], y, Y, dev_yl, dev_yr, ys, yr, 0
    )
    y2 = Ring(
        lambda s, h: R.at[s, c, 0, pl.ds(h * 512, 512), :], y, Y, dev_yl, dev_yr, ys, yr, 6
    )
    x2 = Ring(
        lambda s, h: R.at[pl.ds(2 * h, 2), c, 1, rows(s * XROWS, XROWS), :], x, X, dev_xl, dev_xr, xs, xr, 6
    )

    for copy in along_z:
        copy.wait_recv()
    x1.first()
    y1.first()
    for copy in tabs:
        copy.wait_recv()
    ring_t.first()
    x1.relay()
    y1.relay()
    ring_t.relay()
    x1.low()
    x1.high()
    x1.far()

    def sibling(ref, k):
        return send(ref, ref, ss.at[k], sr.at[k], dev_sib)

    y2.first()
    sib = {}
    sib[0] = sibling(R.at[y, c, 0], 0)
    y1.low()
    y1.high()
    y1.far()
    x2.first()
    sib[1] = sibling(R.at[:, c, 1, rows(x * XROWS, XROWS), :], 1)

    def weight(q):
        return W[pl.ds(pl.multiple_of(q * HALF, HALF), HALF), :]

    def unit_y(yy, cc):
        w = weight((yy * C + cc) * 2)

        def step(i, carry):
            at = rows(i * 256, 256)
            ACC[at, :] += jnp.dot(R[yy, cc, 0, at, :], w, preferred_element_type=jnp.float32)
            return carry

        lax.fori_loop(0, ROWS // 256, step, 0)

    def unit_x(xx, cc):
        at = rows(xx * XROWS, XROWS)

        def step(yy, carry):
            ACC[at, :] += jnp.dot(
                R[yy, cc, 1, at, :], weight((yy * C + cc) * 2 + 1), preferred_element_type=jnp.float32
            )
            return carry

        lax.fori_loop(0, Y, step, 0)

    unit_y(y, c)
    unit_x(x, c)
    sib[0].wait_recv()
    unit_y(y, 1 - c)
    sib[1].wait_recv()
    unit_x(x, 1 - c)
    y2.relay()
    x2.relay()
    y2.low()
    sib[2] = sibling(R.at[yl, c, 0], 2)
    y2.high()
    sib[3] = sibling(R.at[yri, c, 0], 3)
    x2.low()
    sib[4] = sibling(R.at[:, c, 1, rows(xl * XROWS, XROWS), :], 4)
    x2.high()
    sib[5] = sibling(R.at[:, c, 1, rows(xri * XROWS, XROWS), :], 5)
    unit_y(yl, c)
    unit_y(yri, c)
    unit_x(xl, c)
    unit_x(xri, c)
    y2.far()
    sib[6] = sibling(R.at[yo, c, 0], 6)
    x2.far()
    sib[7] = sibling(R.at[:, c, 1, rows(xo * XROWS, XROWS), :], 7)
    unit_y(yo, c)
    unit_x(xo, c)
    for k, (unit, who) in enumerate(
        [(unit_y, yl), (unit_y, yri), (unit_x, xl), (unit_x, xri), (unit_y, yo), (unit_x, xo)]
    ):
        sib[2 + k].wait_recv()
        unit(who, 1 - c)

    def activate(i, carry):
        at = rows(i * 128, 128)
        gate_part = ACC[at, 0:HID]
        up_part = ACC[at, HID:2 * HID]
        HF[y, c, at, :] = (gate_part / (1.0 + jnp.exp(-gate_part)) * up_part).astype(jnp.bfloat16)
        return carry

    lax.fori_loop(0, ROWS // 128, activate, 0)

    def hsib(ref, k):
        return send(ref, ref, hss.at[k], hsr.at[k], dev_sib)

    hring = Ring(lambda s, h: HF.at[s, c, pl.ds(h * 512, 512), :], y, Y, dev_yl, dev_yr, hs, hr, 0)
    hring.first()
    hsibs = [hsib(HF.at[y, c], 0)]
    hring.relay()
    ring_t.low()
    ring_t.high()
    ring_t.far()
    own_down.wait()
    for copy in downs:
        copy.wait_recv()
    hring.low()
    hsibs.append(hsib(HF.at[yl, c], 1))
    hring.high()
    hsibs.append(hsib(HF.at[yri, c], 2))
    hring.far()
    hsibs.append(hsib(HF.at[yo, c], 3))
    for copy in hsibs:
        copy.wait_recv()

    expert = ep.astype(jnp.float32)
    lane = lax.broadcasted_iota(jnp.int32, (XROWS, 128), 1)

    def project(xx):
        at = rows(xx * XROWS, XROWS)
        t = T[at, :].astype(jnp.float32)
        probs = pltpu.roll(t, 128 - TOP, 1) + (pltpu.roll(t, 128 - 2 * TOP, 1) + pltpu.roll(t, 128 - 3 * TOP, 1))
        scale = jnp.sum(jnp.where((lane < TOP) & (t == expert), probs, 0.0), axis=1, keepdims=True)
        total = jnp.zeros((XROWS, SLICE), jnp.float32)
        for yy in range(Y):
            act = jnp.concatenate([HF[yy, 0, at, :], HF[yy, 1, at, :]], axis=1)
            down = DT[2 * yy:2 * yy + 2].reshape(2 * HID, SLICE)
            total += jnp.dot(act, down, preferred_element_type=jnp.float32)
        return total * scale

    def part(xx, keep):
        at = rows(xx * XROWS, XROWS)
        total = project(xx)
        if keep:
            YF[...] = total
        else:
            PB[0, at, :] = total[:, :HALF].astype(jnp.bfloat16)
            PB[1, at, :] = total[:, HALF:].astype(jnp.bfloat16)

    def pb(h, xx):
        return PB.at[h, rows(xx * XROWS, XROWS), :]

    part(xo, False)
    d1 = send(pb(0, xo), XR.at[0], rs.at[0], rr.at[0], dev_xr)
    d2 = send(pb(1, xo), XR.at[1], rs.at[1], rr.at[1], dev_xl)
    part(xri, False)
    d3 = send(pb(1, xri), XR.at[2], rs.at[2], rr.at[2], dev_xr)
    part(xl, False)
    d4 = send(pb(0, xl), XR.at[3], rs.at[3], rr.at[3], dev_xl)
    d1.wait_recv()
    XS[0] = (PB[0, rows(xri * XROWS, XROWS), :].astype(jnp.float32) + XR[0].astype(jnp.float32)).astype(jnp.bfloat16)
    d5 = send(XS.at[0], XR.at[4], rs.at[4], rr.at[4], dev_xr)
    d2.wait_recv()
    XS[1] = (PB[1, rows(xl * XROWS, XROWS), :].astype(jnp.float32) + XR[1].astype(jnp.float32)).astype(jnp.bfloat16)
    d6 = send(XS.at[1], XR.at[5], rs.at[5], rr.at[5], dev_xl)
    part(x, True)
    for copy in (d3, d4, d5, d6):
        copy.wait_recv()
    for h, (one, two) in enumerate(((3, 4), (2, 5))):
        cols = slice(h * HALF, (h + 1) * HALF)
        total = YF[:, cols] + XR[one].astype(jnp.float32) + XR[two].astype(jnp.float32)
        ZS[:, cols] = total
        total = total.astype(jnp.bfloat16)
        for zz in range(Z):
            ZP[zz, :, cols] = total[zz * COL:(zz + 1) * COL]
    back = [
        send(ZP.at[lax.rem(z + d, Z)], ZR.at[d - 1], zzs.at[d - 1], zzr.at[d - 1], zdev[d - 1])
        for d in range(1, Z)
    ]
    for copy in back:
        copy.wait_recv()
    total = ZS[rows(z * COL, COL), :]
    for d in range(1, Z):
        total += ZR[d - 1].astype(jnp.float32)
    total = total.astype(jnp.bfloat16).astype(jnp.float32)
    for r in range(REP):
        FA[r] = total[2 * r:2 * r + 2, :].astype(jnp.bfloat16)
    last = [send(FA.at[r], FB.at[rep], fs.at[i], fr.at[i], at_rep(r)) for i, r in enumerate(rdev)]
    FB[rep] = FA[rep]
    for copy in last:
        copy.wait_recv()
    for r in range(REP):
        out[:, r * SLICE:(r + 1) * SLICE] = FB[r]
    for copy in pending:
        copy.wait_send()


def on_device(
    hidden_state, norm_gain, expert_ids, gate_logits, gate_weight, up_weight, down_weight
):
    exp_logits = jnp.exp(gate_logits)
    gate_probs = exp_logits / jnp.sum(exp_logits, axis=1, keepdims=True)
    hi = lax.reduce_precision(gate_probs, 8, 7)
    mid = lax.reduce_precision(gate_probs - hi, 8, 7)
    low = gate_probs - hi - mid
    table = jnp.concatenate([expert_ids.astype(jnp.float32), hi, mid, low], axis=1)
    table = jnp.pad(table, ((0, 0), (0, 128 - 4 * TOP))).astype(jnp.bfloat16)
    bf, f32 = jnp.bfloat16, jnp.float32
    vmem = pl.BlockSpec(memory_space=pltpu.VMEM)
    hbm = pl.BlockSpec(memory_space=pl.ANY)
    dma = pltpu.SemaphoreType.DMA
    return pl.pallas_call(
        kernel,
        out_shape=jax.ShapeDtypeStruct((COL // REP, D), bf),
        in_specs=[vmem, vmem, vmem, hbm, hbm, hbm],
        out_specs=vmem,
        scratch_shapes=[
            pltpu.VMEM((REP, 2, SLICE), bf),
            pltpu.VMEM((REP, 2, SLICE), bf),
            pltpu.VMEM((COL, SLICE), f32),
            pltpu.VMEM((Y, C, 2, ROWS, HALF), bf),
            pltpu.VMEM((ROWS, 128), bf),
            pltpu.VMEM((D, 2 * HID), bf),
            pltpu.VMEM((ROWS, 2 * HID), f32),
            pltpu.VMEM((Y, C, ROWS, HID), bf),
            pltpu.VMEM((REP, HID, SLICE), bf),
            pltpu.VMEM((XROWS, SLICE), f32),
            pltpu.VMEM((2, ROWS, HALF), bf),
            pltpu.VMEM((6, XROWS, HALF), bf),
            pltpu.VMEM((2, XROWS, HALF), bf),
            pltpu.VMEM((XROWS, SLICE), f32),
            pltpu.VMEM((Z, COL, SLICE), bf),
            pltpu.VMEM((Z - 1, COL, SLICE), bf),
            pltpu.VMEM((REP, 2, SLICE), bf),
            pltpu.VMEM((REP, 2, SLICE), bf),
            dma((3,)),
            dma((REP - 1,)), dma((REP - 1,)),
            dma((REP - 1,)), dma((REP - 1,)),
            dma((Z - 1,)), dma((Z - 1,)),
            dma((Z - 1,)), dma((Z - 1,)),
            dma((12,)), dma((12,)),
            dma((12,)), dma((12,)),
            dma((8,)), dma((8,)),
            dma((6,)), dma((6,)),
            dma((6,)), dma((6,)),
            dma((4,)), dma((4,)),
            dma((6,)), dma((6,)),
            dma((Z - 1,)), dma((Z - 1,)),
            dma((REP - 1,)), dma((REP - 1,)),
        ],
        compiler_params=pltpu.CompilerParams(
            collective_id=0, has_side_effects=True, vmem_limit_bytes=56 * 1024 * 1024
        ),
    )(hidden_state, norm_gain.reshape(1, D), table, gate_weight, up_weight, down_weight)


def solution(mesh):
    placed = (
        P(("ep", "rep"), None),
        P(),
        P("ep", None),
        P("ep", None),
        P("ep", None, "rep"),
        P("ep", None, "rep"),
        P("ep", "rep", None),
    )
    return jax.shard_map(
        on_device, mesh=mesh, in_specs=placed, out_specs=P(("ep", "rep"), None), check_vma=False
    )
```

```python
import jax
import jax.numpy as jnp
from jax import lax
from jax.experimental import pallas as pl
from jax.experimental.pallas import tpu as pltpu
from jax.sharding import PartitionSpec as P

epsilon = 1e-06
MESH = pl.DeviceIdType.MESH
Y, C, X, Z = 4, 2, 4, 16
ZQ = 4
REP = Y * C
COL = 16
TOP = 8
ROWS = X * Z * COL
XROWS = Z * COL
D = 4096
SLICE = D // REP
HALF = SLICE // 2
HID = 128
SENDS = 240


def kernel(
    hid, gain, ids, logits, gw, uw, dw, out,
    SA, SB, BF, TB, R, T, W, ACC, HF, DT, PB, ZA, ZB, FA, FB,
    lsem, ssem, rsem,
):
    rep = lax.axis_index("rep")
    ep = lax.axis_index("ep")
    y, c = rep // C, lax.rem(rep, C)
    x, z = ep // Z, lax.rem(ep, Z)
    zhi, zlo = z // ZQ, lax.rem(z, ZQ)
    f32, bf16 = jnp.float32, jnp.bfloat16

    def wrap(v, n):
        return lax.rem(v + n, n)

    def at_rep(r):
        return {"rep": r, "ep": ep}

    def at_ep(e):
        return {"rep": rep, "ep": e}

    def at_z(d):
        return at_ep(x * Z + wrap(z + d, Z))

    xl, xri, xo = wrap(x - 1, X), wrap(x + 1, X), wrap(x + 2, X)
    yl, yri, yo = wrap(y - 1, Y), wrap(y + 1, Y), wrap(y + 2, Y)
    dev_x = (at_ep(xl * Z + z), at_ep(xri * Z + z))
    dev_y = (at_rep(yl * C + c), at_rep(yri * C + c))
    dev_sib = at_rep(y * C + 1 - c)
    rdev = [lax.rem(rep + d, REP) for d in range(1, REP)]

    pending = []

    def send(src, dst, dev):
        k = len(pending)
        copy = pltpu.make_async_remote_copy(
            src_ref=src, dst_ref=dst, send_sem=ssem.at[k], recv_sem=rsem.at[k], device_id=dev, device_id_type=MESH
        )
        copy.start()
        pending.append(copy)
        return copy

    def share(ref, dev):
        return send(ref, ref, dev)

    barrier = pltpu.get_barrier_semaphore()
    def at_class(k, r):
        return {"rep": r, "ep": x * Z + wrap(zhi + k, ZQ) * ZQ + zlo}

    spread = [(k, at_class(k, lax.rem(rep + d, REP)), d) for k in range(ZQ) for d in range(REP) if k or d]
    def at_xz(xx, d):
        return at_ep(xx * Z + wrap(z + d, Z))

    partners = [dev for _, dev, _ in spread]
    partners += [at_xz(xx, d) for xx in (xl, xri, xo) for d in (0, 1, -1, 2, -2)]
    partners += [at_z(d) for d in (1, -1, 2, -2)]
    for dev in partners:
        pl.semaphore_signal(barrier, inc=1, device_id=dev, device_id_type=MESH)
    loads = [
        pltpu.make_async_copy(gw.at[0], W.at[:, 0:HID], lsem.at[0]),
        pltpu.make_async_copy(uw.at[0], W.at[:, HID:2 * HID], lsem.at[1]),
    ]
    for load in loads:
        load.start()

    values = hid[...].astype(f32)
    inverse_rms = lax.rsqrt(jnp.mean(values * values, axis=-1, keepdims=True) + epsilon)
    normed = (values * inverse_rms * gain[...]).astype(bf16)
    for r in range(REP):
        SA[r] = normed[:, r * SLICE:(r + 1) * SLICE]
    exp_logits = jnp.exp(logits[...])
    probs = exp_logits / jnp.sum(exp_logits, axis=1, keepdims=True)
    high = probs.astype(bf16).astype(f32)
    middle = (probs - high).astype(bf16).astype(f32)
    TB[...] = jnp.zeros_like(TB)
    TB[:, 0:TOP] = ids[...].astype(f32)
    TB[:, TOP:2 * TOP] = high
    TB[:, 2 * TOP:3 * TOP] = middle
    TB[:, 3 * TOP:4 * TOP] = probs - high - middle
    T[x, zhi, zlo] = TB[...].astype(bf16)
    pl.semaphore_wait(barrier, len(partners))

    first = [send(SA.at[lax.rem(rep + d, REP)], SB.at[zhi, rep], dev) for _, dev, d in spread]
    tlevel = [share(T.at[x, zhi, zlo], at_class(k, rep)) for k in range(1, ZQ)]
    def down_slice(r):
        return dw.at[0, :, pl.ds(pl.multiple_of(r * SLICE, SLICE), SLICE)]

    downs = [send(down_slice(r), DT.at[rep], at_rep(r)) for r in rdev]
    own_down = pltpu.make_async_copy(down_slice(rep), DT.at[rep], lsem.at[2])
    own_down.start()
    SB[zhi, rep] = SA[rep]
    for copy in first:
        copy.wait_recv()
    q0 = rep * 2
    for k in range(ZQ):
        for r in range(REP):
            BF[k, 2 * r:2 * r + 2, :] = SB[k, r].astype(f32)
    for k in range(ZQ):
        block = BF[k].astype(bf16)
        R[q0, x, k, zlo] = block[:, :HALF]
        R[q0 + 1, x, k, zlo] = block[:, HALF:]
    both = R.at[pl.ds(q0, 2), x, :, zlo]
    level = [share(both, at_z(1)), share(both, at_z(-1))]
    level += [share(R.at[q0, x, :, zlo], at_z(2)), share(R.at[q0 + 1, x, :, zlo], at_z(-2))]
    for copy in tlevel:
        copy.wait_recv()
    tlevel = [share(T.at[x, :, zlo], at_z(d)) for d in (1, -1, 2)]

    class Ring:
        def __init__(self, view, me, n, devs):
            self.view, self.me, self.devs = view, me, devs
            self.lo, self.hi = wrap(me - 1, n), wrap(me + 1, n)

        def put(self, who, half, side):
            return share(self.view(who, half), self.devs[side])

        def first(self):
            self.ra = self.put(self.me, 0, 1)
            self.lb = self.put(self.me, 1, 0)
            self.rb = self.put(self.me, 1, 1)
            self.la = self.put(self.me, 0, 0)
            return self

        def relay(self):
            self.ra.wait_recv()
            self.oa = self.put(self.lo, 0, 1)
            self.lb.wait_recv()
            self.ob = self.put(self.hi, 1, 0)

        def low(self):
            self.rb.wait_recv()

        def high(self):
            self.la.wait_recv()

        def far(self):
            self.oa.wait_recv()
            self.ob.wait_recv()

    def piece(yy, h, xx):
        return R.at[(yy * C + c) * 2 + h, xx]

    def cut(ref, half):
        return ref.at[pl.ds(2 * half, 2)]

    def along_y(h, xx):
        return Ring(lambda s, half: cut(piece(s, h, xx), half), y, Y, dev_y)

    def along_x(h, yy):
        return Ring(lambda s, half: cut(piece(yy, h, s), half), x, X, dev_x)

    sib = {}

    def forward(yy, h, xx, name):
        sib[name + (h,)] = share(piece(yy, h, xx), dev_sib)

    for load in loads:
        load.wait()
    for copy in level:
        copy.wait_recv()
    x1 = along_x(0, y).first()
    y1 = along_y(1, x).first()
    y2 = {"own": along_y(0, x).first()}
    x2 = {"own": along_x(1, y).first()}
    for copy in tlevel:
        copy.wait_recv()
    ring_t = Ring(lambda s, h: T.at[s, pl.ds(2 * h, 2)], x, X, dev_x).first()
    forward(y, 0, x, ("own", "own"))
    forward(y, 1, x, ("own", "own"))
    x1.relay()
    y1.relay()
    x1.low()
    y2["low"] = along_y(0, xl).first()
    y1.low()
    x2["low"] = along_x(1, yl).first()
    x1.high()
    y2["high"] = along_y(0, xri).first()
    y1.high()
    x2["high"] = along_x(1, yri).first()
    forward(y, 0, xl, ("own", "low"))
    forward(y, 0, xri, ("own", "high"))
    forward(yl, 1, x, ("low", "own"))
    forward(yri, 1, x, ("high", "own"))
    y2["own"].relay()
    x2["own"].relay()
    x1.far()
    y2["far"] = along_y(0, xo).first()
    y1.far()
    x2["far"] = along_x(1, yo).first()
    forward(y, 0, xo, ("own", "far"))
    forward(yo, 1, x, ("far", "own"))
    xname = {"own": x, "low": xl, "high": xri, "far": xo}
    yname = {"own": y, "low": yl, "high": yri, "far": yo}

    def near_y(g):
        y2[g].low()
        forward(yl, 0, xname[g], ("low", g))
        y2[g].high()
        forward(yri, 0, xname[g], ("high", g))

    def far_y(g):
        y2[g].far()
        forward(yo, 0, xname[g], ("far", g))

    def near_x(g):
        x2[g].low()
        forward(yname[g], 1, xl, (g, "low"))
        x2[g].high()
        forward(yname[g], 1, xri, (g, "high"))

    def far_x(g):
        x2[g].far()
        forward(yname[g], 1, xo, (g, "far"))

    def gathered(g):
        for name in list(sib):
            if name[1] == g:
                sib.pop(name).wait_recv()

    def gateup(xx):
        total = None
        for q in range(2 * REP):
            part = jnp.dot(
                R[q, xx].reshape(XROWS, HALF), W[q * HALF:(q + 1) * HALF, :], preferred_element_type=f32
            )
            total = part if total is None else total + part
        ACC[...] = total
        for i in range(2):
            at = slice(i * 128, (i + 1) * 128)
            gate_part = ACC[at, 0:HID]
            up_part = ACC[at, HID:2 * HID]
            HF[y, c, xx, at, :] = (gate_part / (1.0 + jnp.exp(-gate_part)) * up_part).astype(bf16)

    hrings = {}
    hsibs = {}

    def hstart(g):
        xx = xname[g]
        hrings[g] = Ring(lambda s, half: HF.at[s, c, xx, pl.ds(half * 128, 128)], y, Y, dev_y).first()
        hsibs[g] = [share(HF.at[y, c, xx], dev_sib)]

    def hnear(g):
        xx = xname[g]
        hrings[g].relay()
        hrings[g].low()
        hsibs[g].append(share(HF.at[yl, c, xx], dev_sib))
        hrings[g].high()
        hsibs[g].append(share(HF.at[yri, c, xx], dev_sib))

    def hfar(g):
        hrings[g].far()
        hsibs[g].append(share(HF.at[yo, c, xname[g]], dev_sib))

    def hdone(g):
        for copy in hsibs[g]:
            copy.wait_recv()

    near_y("own")
    near_x("own")
    y2["low"].relay()
    x2["low"].relay()
    y2["high"].relay()
    x2["high"].relay()
    far_y("own")
    far_x("own")
    gathered("own")
    gateup(x)
    hstart("own")
    near_y("low")
    near_x("low")
    near_y("high")
    near_x("high")
    y2["far"].relay()
    x2["far"].relay()
    far_y("low")
    far_x("low")
    far_y("high")
    far_x("high")
    hnear("own")
    near_y("far")
    near_x("far")
    gathered("low")
    gateup(xl)
    hstart("low")
    gathered("high")
    gateup(xri)
    hstart("high")
    far_y("far")
    far_x("far")
    ring_t.relay()
    hfar("own")
    hnear("low")
    hnear("high")
    gathered("far")
    gateup(xo)
    hlast = [share(HF.at[y, c, xo], at_rep(to * C + c)) for to in (yl, yri, yo)]
    hsibs["far"] = [share(HF.at[y, c, xo], dev_sib)]
    ring_t.low()
    ring_t.high()
    ring_t.far()
    own_down.wait()
    for copy in downs:
        copy.wait_recv()

    expert = ep.astype(f32)
    lane = lax.broadcasted_iota(jnp.int32, (XROWS, 128), 1)

    def project(xx):
        t = T[xx].reshape(XROWS, 128).astype(f32)
        parts = pltpu.roll(t, 128 - TOP, 1) + (pltpu.roll(t, 128 - 2 * TOP, 1) + pltpu.roll(t, 128 - 3 * TOP, 1))
        scale = jnp.sum(jnp.where((lane < TOP) & (t == expert), parts, 0.0), axis=1, keepdims=True)
        total = jnp.zeros((XROWS, SLICE), f32)
        for yy in range(Y):
            act = jnp.concatenate([HF[yy, 0, xx], HF[yy, 1, xx]], axis=1)
            down = DT[2 * yy:2 * yy + 2].reshape(2 * HID, SLICE)
            total += jnp.dot(act, down, preferred_element_type=f32)
        return total * scale

    def part(xx):
        total = project(xx).astype(bf16)
        for h in range(2):
            for zz in range(Z):
                PB[xx, h, zz % ZQ, zz // ZQ] = total[zz * COL:(zz + 1) * COL, h * HALF:(h + 1) * HALF]

    scattered = []

    def scatter(xx, own):
        if own:
            ZA[x, 0] = PB[x, :, zlo]
        else:
            scattered.append(send(PB.at[xx, :, zlo], ZA.at[x, 0], at_xz(xx, 0)))
        for k, d in ((1, 1), (2, -1)):
            scattered.append(send(PB.at[xx, :, wrap(zlo + d, ZQ)], ZA.at[x, k], at_xz(xx, d)))
        for k, d in ((0, 2), (1, -2)):
            scattered.append(send(PB.at[xx, k, wrap(zlo + 2, ZQ)], ZB.at[x, k], at_xz(xx, d)))

    hfar("low")
    hfar("high")
    hdone("low")
    part(xl)
    scatter(xl, False)
    hdone("high")
    part(xri)
    scatter(xri, False)
    hdone("own")
    part(x)
    scatter(x, True)
    for copy, who in zip(hlast, (yri, yl, yo)):
        copy.wait_recv()
        hsibs["far"].append(share(HF.at[who, c, xo], dev_sib))
    hdone("far")
    part(xo)
    scatter(xo, False)
    for copy in scattered:
        copy.wait_recv()
    for h in range(2):
        total = jnp.zeros((ZQ, COL, HALF), f32)
        for xx in range(X):
            for k in range(3):
                total += ZA[xx, k, h].astype(f32)
            total += ZB[xx, h].astype(f32)
        for k in range(ZQ):
            BF[k, :, h * HALF:(h + 1) * HALF] = total[k]
    for k in range(ZQ):
        for r in range(REP):
            FA[k, r] = BF[k, 2 * r:2 * r + 2, :].astype(bf16)
    last = [
        send(FA.at[wrap(zhi + k, ZQ), lax.rem(rep + d, REP)], FB.at[zhi, rep], dev) for k, dev, d in spread
    ]
    FB[zhi, rep] = FA[zhi, rep]
    for copy in last:
        copy.wait_recv()
    for r in range(REP):
        total = FB[0, r].astype(f32)
        for k in range(1, ZQ):
            total += FB[k, r].astype(f32)
        out[:, r * SLICE:(r + 1) * SLICE] = total.astype(bf16)
    for copy in pending:
        copy.wait_send()


def on_device(
    hidden_state, norm_gain, expert_ids, gate_logits, gate_weight, up_weight, down_weight
):
    bf, f32 = jnp.bfloat16, jnp.float32
    vmem = pl.BlockSpec(memory_space=pltpu.VMEM)
    hbm = pl.BlockSpec(memory_space=pl.ANY)
    dma = pltpu.SemaphoreType.DMA
    return pl.pallas_call(
        kernel,
        out_shape=jax.ShapeDtypeStruct((COL // REP, D), bf),
        in_specs=[vmem, vmem, vmem, vmem, hbm, hbm, hbm],
        out_specs=vmem,
        scratch_shapes=[
            pltpu.VMEM((REP, 2, SLICE), bf),
            pltpu.VMEM((ZQ, REP, 2, SLICE), bf),
            pltpu.VMEM((ZQ, COL, SLICE), f32),
            pltpu.VMEM((COL, 128), f32),
            pltpu.VMEM((2 * REP, X, ZQ, ZQ, COL, HALF), bf),
            pltpu.VMEM((X, ZQ, ZQ, COL, 128), bf),
            pltpu.VMEM((D, 2 * HID), bf),
            pltpu.VMEM((XROWS, 2 * HID), f32),
            pltpu.VMEM((Y, C, X, XROWS, HID), bf),
            pltpu.VMEM((REP, HID, SLICE), bf),
            pltpu.VMEM((X, 2, ZQ, ZQ, COL, HALF), bf),
            pltpu.VMEM((X, 3, 2, ZQ, COL, HALF), bf),
            pltpu.VMEM((X, 2, ZQ, COL, HALF), bf),
            pltpu.VMEM((ZQ, REP, 2, SLICE), bf),
            pltpu.VMEM((ZQ, REP, 2, SLICE), bf),
            dma((3,)),
            dma((SENDS,)),
            dma((SENDS,)),
        ],
        compiler_params=pltpu.CompilerParams(
            collective_id=0, has_side_effects=True, vmem_limit_bytes=56 * 1024 * 1024
        ),
    )(hidden_state, norm_gain.reshape(1, D), expert_ids, gate_logits, gate_weight, up_weight, down_weight)


def solution(mesh):
    placed = (
        P(("ep", "rep"), None),
        P(),
        P("ep", None),
        P("ep", None),
        P("ep", None, "rep"),
        P("ep", None, "rep"),
        P("ep", "rep", None),
    )
    return jax.shard_map(
        on_device, mesh=mesh, in_specs=placed, out_specs=P(("ep", "rep"), None), check_vma=False
    )
```

```python
import jax
import jax.numpy as jnp
from jax import lax
from jax.experimental import pallas as pl
from jax.experimental.pallas import tpu as pltpu
from jax.sharding import PartitionSpec as P

epsilon = 1e-06
MESH = pl.DeviceIdType.MESH
Y, C, X, Z = 4, 2, 4, 16
ZQ = 4
REP = Y * C
COL = 16
TOP = 8
ROWS = X * Z * COL
XROWS = Z * COL
D = 4096
SLICE = D // REP
HALF = SLICE // 2
HID = 128
SENDS = 240


def kernel(
    hid, gain, ids, logits, gw, uw, dw, out,
    SA, SB, BF, R, T, W, ACC, HF, DT, PB, ZA, ZB, FA, FB,
    lsem, ssem, rsem,
):
    rep = lax.axis_index("rep")
    ep = lax.axis_index("ep")
    y, c = rep // C, lax.rem(rep, C)
    x, z = ep // Z, lax.rem(ep, Z)
    zhi, zlo = z // ZQ, lax.rem(z, ZQ)
    f32, bf16 = jnp.float32, jnp.bfloat16

    def wrap(v, n):
        return lax.rem(v + n, n)

    def at_rep(r):
        return {"rep": r, "ep": ep}

    def at_ep(e):
        return {"rep": rep, "ep": e}

    def at_z(d):
        return at_ep(x * Z + wrap(z + d, Z))

    xl, xri, xo = wrap(x - 1, X), wrap(x + 1, X), wrap(x + 2, X)
    yl, yri, yo = wrap(y - 1, Y), wrap(y + 1, Y), wrap(y + 2, Y)
    dev_x = (at_ep(xl * Z + z), at_ep(xri * Z + z))
    dev_y = (at_rep(yl * C + c), at_rep(yri * C + c))
    dev_sib = at_rep(y * C + 1 - c)
    rdev = [lax.rem(rep + d, REP) for d in range(1, REP)]

    pending = []

    def send(src, dst, dev):
        k = len(pending)
        copy = pltpu.make_async_remote_copy(
            src_ref=src, dst_ref=dst, send_sem=ssem.at[k], recv_sem=rsem.at[k], device_id=dev, device_id_type=MESH
        )
        copy.start()
        pending.append(copy)
        return copy

    def share(ref, dev):
        return send(ref, ref, dev)

    barrier = pltpu.get_barrier_semaphore()
    def at_class(k, r):
        return {"rep": r, "ep": x * Z + wrap(zhi + k, ZQ) * ZQ + zlo}

    spread = [(k, at_class(k, lax.rem(rep + d, REP)), d) for k in range(ZQ) for d in range(REP) if k or d]
    def at_xz(xx, d):
        return at_ep(xx * Z + wrap(z + d, Z))

    partners = [dev for _, dev, _ in spread]
    partners += [at_xz(xx, d) for xx in (xl, xri, xo) for d in (0, 1, -1, 2, -2)]
    partners += [at_z(d) for d in (1, -1, 2, -2)]
    for dev in partners:
        pl.semaphore_signal(barrier, inc=1, device_id=dev, device_id_type=MESH)
    loads = [
        pltpu.make_async_copy(gw.at[0], W.at[:, 0:HID], lsem.at[0]),
        pltpu.make_async_copy(uw.at[0], W.at[:, HID:2 * HID], lsem.at[1]),
    ]
    for load in loads:
        load.start()

    values = hid[...].astype(f32)
    inverse_rms = lax.rsqrt(jnp.mean(values * values, axis=-1, keepdims=True) + epsilon)
    normed = (values * inverse_rms * gain[...]).astype(bf16)
    for r in range(REP):
        SA[r] = normed[:, r * SLICE:(r + 1) * SLICE]
    exp_logits = jnp.exp(logits[...])
    probs = exp_logits / jnp.sum(exp_logits, axis=0, keepdims=True)
    high = probs.astype(bf16).astype(f32)
    middle = (probs - high).astype(bf16).astype(f32)
    stacked = jnp.concatenate([ids[...].astype(f32), high, middle, probs - high - middle], axis=0)
    shape = (4 * TOP, 128)
    pick = lax.broadcasted_iota(jnp.int32, shape, 0) == lax.broadcasted_iota(jnp.int32, shape, 1)
    T[x, zhi, zlo] = lax.dot_general(
        stacked.astype(bf16), pick.astype(f32).astype(bf16), (((0,), (0,)), ((), ())), preferred_element_type=f32
    ).astype(bf16)
    pl.semaphore_wait(barrier, len(partners))

    first = [send(SA.at[lax.rem(rep + d, REP)], SB.at[zhi, rep], dev) for _, dev, d in spread]
    tlevel = [share(T.at[x, zhi, zlo], at_class(k, rep)) for k in range(1, ZQ)]
    def down_slice(r):
        return dw.at[0, :, pl.ds(pl.multiple_of(r * SLICE, SLICE), SLICE)]

    downs = [send(down_slice(r), DT.at[rep], at_rep(r)) for r in rdev]
    own_down = pltpu.make_async_copy(down_slice(rep), DT.at[rep], lsem.at[2])
    own_down.start()
    SB[zhi, rep] = SA[rep]
    for copy in first:
        copy.wait_recv()
    q0 = rep * 2
    for k in range(ZQ):
        for r in range(REP):
            BF[k, 2 * r:2 * r + 2, :] = SB[k, r].astype(f32)
    for k in range(ZQ):
        block = BF[k].astype(bf16)
        R[q0, x, k, zlo] = block[:, :HALF]
        R[q0 + 1, x, k, zlo] = block[:, HALF:]
    both = R.at[pl.ds(q0, 2), x, :, zlo]
    level = [share(both, at_z(1)), share(both, at_z(-1))]
    level += [share(R.at[q0, x, :, zlo], at_z(2)), share(R.at[q0 + 1, x, :, zlo], at_z(-2))]
    for copy in tlevel:
        copy.wait_recv()
    tlevel = [share(T.at[x, :, zlo], at_z(d)) for d in (1, -1, 2)]

    class Ring:
        def __init__(self, view, me, n, devs):
            self.view, self.me, self.devs = view, me, devs
            self.lo, self.hi = wrap(me - 1, n), wrap(me + 1, n)

        def put(self, who, half, side):
            return share(self.view(who, half), self.devs[side])

        def first(self):
            self.ra = self.put(self.me, 0, 1)
            self.lb = self.put(self.me, 1, 0)
            self.rb = self.put(self.me, 1, 1)
            self.la = self.put(self.me, 0, 0)
            return self

        def relay(self):
            self.ra.wait_recv()
            self.oa = self.put(self.lo, 0, 1)
            self.lb.wait_recv()
            self.ob = self.put(self.hi, 1, 0)

        def low(self):
            self.rb.wait_recv()

        def high(self):
            self.la.wait_recv()

        def far(self):
            self.oa.wait_recv()
            self.ob.wait_recv()

    def piece(yy, h, xx):
        return R.at[(yy * C + c) * 2 + h, xx]

    def cut(ref, half):
        return ref.at[pl.ds(2 * half, 2)]

    def along_y(h, xx):
        return Ring(lambda s, half: cut(piece(s, h, xx), half), y, Y, dev_y)

    def along_x(h, yy):
        return Ring(lambda s, half: cut(piece(yy, h, s), half), x, X, dev_x)

    sib = {}

    def forward(yy, h, xx, name):
        sib[name + (h,)] = share(piece(yy, h, xx), dev_sib)

    for load in loads:
        load.wait()
    for copy in level:
        copy.wait_recv()
    x1 = along_x(0, y).first()
    y1 = along_y(1, x).first()
    y2 = {"own": along_y(0, x).first()}
    x2 = {"own": along_x(1, y).first()}
    forward(y, 0, x, ("own", "own"))
    forward(y, 1, x, ("own", "own"))
    x1.relay()
    y1.relay()
    x1.low()
    y2["low"] = along_y(0, xl).first()
    y1.low()
    x2["low"] = along_x(1, yl).first()
    x1.high()
    y2["high"] = along_y(0, xri).first()
    y1.high()
    x2["high"] = along_x(1, yri).first()
    forward(y, 0, xl, ("own", "low"))
    forward(y, 0, xri, ("own", "high"))
    forward(yl, 1, x, ("low", "own"))
    forward(yri, 1, x, ("high", "own"))
    y2["own"].relay()
    x2["own"].relay()
    x1.far()
    y2["far"] = along_y(0, xo).first()
    y1.far()
    x2["far"] = along_x(1, yo).first()
    forward(y, 0, xo, ("own", "far"))
    forward(yo, 1, x, ("far", "own"))
    xname = {"own": x, "low": xl, "high": xri, "far": xo}
    yname = {"own": y, "low": yl, "high": yri, "far": yo}

    def near_y(g):
        y2[g].low()
        forward(yl, 0, xname[g], ("low", g))
        y2[g].high()
        forward(yri, 0, xname[g], ("high", g))

    def far_y(g):
        y2[g].far()
        forward(yo, 0, xname[g], ("far", g))

    def near_x(g):
        x2[g].low()
        forward(yname[g], 1, xl, (g, "low"))
        x2[g].high()
        forward(yname[g], 1, xri, (g, "high"))

    def far_x(g):
        x2[g].far()
        forward(yname[g], 1, xo, (g, "far"))

    def gathered(g):
        for name in list(sib):
            if name[1] == g:
                sib.pop(name).wait_recv()

    def gateup(xx):
        total = None
        for q in range(2 * REP):
            part = jnp.dot(
                R[q, xx].reshape(XROWS, HALF), W[q * HALF:(q + 1) * HALF, :], preferred_element_type=f32
            )
            total = part if total is None else total + part
        ACC[...] = total
        for i in range(2):
            at = slice(i * 128, (i + 1) * 128)
            gate_part = ACC[at, 0:HID]
            up_part = ACC[at, HID:2 * HID]
            HF[y, c, xx, at, :] = (gate_part / (1.0 + jnp.exp(-gate_part)) * up_part).astype(bf16)

    hrings = {}
    hsibs = {}

    def hstart(g):
        xx = xname[g]
        hrings[g] = Ring(lambda s, half: HF.at[s, c, xx, pl.ds(half * 128, 128)], y, Y, dev_y).first()
        hsibs[g] = [share(HF.at[y, c, xx], dev_sib)]

    def hnear(g):
        xx = xname[g]
        hrings[g].relay()
        hrings[g].low()
        hsibs[g].append(share(HF.at[yl, c, xx], dev_sib))
        hrings[g].high()
        hsibs[g].append(share(HF.at[yri, c, xx], dev_sib))

    def hfar(g):
        hrings[g].far()
        hsibs[g].append(share(HF.at[yo, c, xname[g]], dev_sib))

    def hdone(g):
        for copy in hsibs[g]:
            copy.wait_recv()

    for copy in tlevel:
        copy.wait_recv()
    ring_t = Ring(lambda s, h: T.at[s, pl.ds(2 * h, 2)], x, X, dev_x).first()
    near_y("own")
    near_x("own")
    y2["low"].relay()
    x2["low"].relay()
    y2["high"].relay()
    x2["high"].relay()
    far_y("own")
    far_x("own")
    gathered("own")
    gateup(x)
    hstart("own")
    near_y("low")
    near_x("low")
    near_y("high")
    near_x("high")
    y2["far"].relay()
    x2["far"].relay()
    far_y("low")
    far_x("low")
    far_y("high")
    far_x("high")
    hnear("own")
    near_y("far")
    near_x("far")
    gathered("low")
    gateup(xl)
    hstart("low")
    gathered("high")
    gateup(xri)
    hstart("high")
    far_y("far")
    far_x("far")
    ring_t.relay()
    hfar("own")
    hnear("low")
    hnear("high")
    gathered("far")
    gateup(xo)
    hlast = [share(HF.at[y, c, xo], at_rep(to * C + c)) for to in (yo, yl, yri)]
    hsibs["far"] = [share(HF.at[y, c, xo], dev_sib)]
    ring_t.low()
    ring_t.high()
    ring_t.far()
    own_down.wait()
    for copy in downs:
        copy.wait_recv()

    expert = ep.astype(f32)
    lane = lax.broadcasted_iota(jnp.int32, (XROWS, 128), 1)

    def project(xx):
        t = T[xx].reshape(XROWS, 128).astype(f32)
        parts = pltpu.roll(t, 128 - TOP, 1) + (pltpu.roll(t, 128 - 2 * TOP, 1) + pltpu.roll(t, 128 - 3 * TOP, 1))
        scale = jnp.sum(jnp.where((lane < TOP) & (t == expert), parts, 0.0), axis=1, keepdims=True)
        total = jnp.zeros((XROWS, SLICE), f32)
        for yy in range(Y):
            act = jnp.concatenate([HF[yy, 0, xx], HF[yy, 1, xx]], axis=1)
            down = DT[2 * yy:2 * yy + 2].reshape(2 * HID, SLICE)
            total += jnp.dot(act, down, preferred_element_type=f32)
        return total * scale

    def part(xx):
        total = project(xx).astype(bf16)
        for h in range(2):
            for zz in range(Z):
                PB[xx, h, zz % ZQ, zz // ZQ] = total[zz * COL:(zz + 1) * COL, h * HALF:(h + 1) * HALF]

    scattered = []

    def scatter(xx, own):
        if own:
            ZA[x, 0] = PB[x, :, zlo]
        else:
            scattered.append(send(PB.at[xx, :, zlo], ZA.at[x, 0], at_xz(xx, 0)))
        for k, d in ((1, 1), (2, -1)):
            scattered.append(send(PB.at[xx, :, wrap(zlo + d, ZQ)], ZA.at[x, k], at_xz(xx, d)))
        for k, d in ((0, 2), (1, -2)):
            scattered.append(send(PB.at[xx, k, wrap(zlo + 2, ZQ)], ZB.at[x, k], at_xz(xx, d)))

    hfar("low")
    hfar("high")
    hdone("low")
    part(xl)
    scatter(xl, False)
    hdone("high")
    part(xri)
    scatter(xri, False)
    hdone("own")
    part(x)
    scatter(x, True)
    for copy, who in zip(hlast[1:] + hlast[:1], (yri, yl, yo)):
        copy.wait_recv()
        hsibs["far"].append(share(HF.at[who, c, xo], dev_sib))
    hdone("far")
    part(xo)
    scatter(xo, False)
    for copy in scattered:
        copy.wait_recv()
    for h in range(2):
        total = jnp.zeros((ZQ, COL, HALF), f32)
        for xx in range(X):
            for k in range(3):
                total += ZA[xx, k, h].astype(f32)
            total += ZB[xx, h].astype(f32)
        for k in range(ZQ):
            BF[k, :, h * HALF:(h + 1) * HALF] = total[k]
    for k in range(ZQ):
        for r in range(REP):
            FA[k, r] = BF[k, 2 * r:2 * r + 2, :].astype(bf16)
    last = [
        send(FA.at[wrap(zhi + k, ZQ), lax.rem(rep + d, REP)], FB.at[zhi, rep], dev) for k, dev, d in spread
    ]
    FB[zhi, rep] = FA[zhi, rep]
    for copy in pending[:-len(last)]:
        copy.wait_send()
    for copy in last:
        copy.wait_recv()
    for r in range(REP):
        total = FB[0, r].astype(f32)
        for k in range(1, ZQ):
            total += FB[k, r].astype(f32)
        out[:, r * SLICE:(r + 1) * SLICE] = total.astype(bf16)
    for copy in last:
        copy.wait_send()


def on_device(
    hidden_state, norm_gain, expert_ids, gate_logits, gate_weight, up_weight, down_weight
):
    bf, f32 = jnp.bfloat16, jnp.float32
    vmem = pl.BlockSpec(memory_space=pltpu.VMEM)
    hbm = pl.BlockSpec(memory_space=pl.ANY)
    dma = pltpu.SemaphoreType.DMA
    return pl.pallas_call(
        kernel,
        out_shape=jax.ShapeDtypeStruct((COL // REP, D), bf),
        in_specs=[vmem, vmem, vmem, vmem, hbm, hbm, hbm],
        out_specs=vmem,
        scratch_shapes=[
            pltpu.VMEM((REP, 2, SLICE), bf),
            pltpu.VMEM((ZQ, REP, 2, SLICE), bf),
            pltpu.VMEM((ZQ, COL, SLICE), f32),
            pltpu.VMEM((2 * REP, X, ZQ, ZQ, COL, HALF), bf),
            pltpu.VMEM((X, ZQ, ZQ, COL, 128), bf),
            pltpu.VMEM((D, 2 * HID), bf),
            pltpu.VMEM((XROWS, 2 * HID), f32),
            pltpu.VMEM((Y, C, X, XROWS, HID), bf),
            pltpu.VMEM((REP, HID, SLICE), bf),
            pltpu.VMEM((X, 2, ZQ, ZQ, COL, HALF), bf),
            pltpu.VMEM((X, 3, 2, ZQ, COL, HALF), bf),
            pltpu.VMEM((X, 2, ZQ, COL, HALF), bf),
            pltpu.VMEM((ZQ, REP, 2, SLICE), bf),
            pltpu.VMEM((ZQ, REP, 2, SLICE), bf),
            dma((3,)),
            dma((SENDS,)),
            dma((SENDS,)),
        ],
        compiler_params=pltpu.CompilerParams(
            collective_id=0, has_side_effects=True, vmem_limit_bytes=56 * 1024 * 1024
        ),
    )(hidden_state, norm_gain.reshape(1, D), expert_ids.T, gate_logits.T, gate_weight, up_weight, down_weight)


def solution(mesh):
    placed = (
        P(("ep", "rep"), None),
        P(),
        P("ep", None),
        P("ep", None),
        P("ep", None, "rep"),
        P("ep", None, "rep"),
        P("ep", "rep", None),
    )
    return jax.shard_map(
        on_device, mesh=mesh, in_specs=placed, out_specs=P(("ep", "rep"), None), check_vma=False
    )
```

```python
import jax
import jax.numpy as jnp
from jax import lax
from jax.experimental import pallas as pl
from jax.experimental.pallas import tpu as pltpu
from jax.sharding import PartitionSpec as P

epsilon = 1e-06
MESH = pl.DeviceIdType.MESH
Y, C, X, Z = 4, 2, 4, 16
ZQ = 4
REP = Y * C
COL = 16
TOP = 8
ROWS = X * Z * COL
XROWS = Z * COL
D = 4096
SLICE = D // REP
HALF = SLICE // 2
HID = 128
SENDS = 240


def kernel(
    hid, gain, ids, logits, gw, uw, dw, out,
    SA, SB, BF, R, T, W, ACC, HF, DT, PB, ZA, ZB, FA, FB,
    lsem, ssem, rsem,
):
    rep = lax.axis_index("rep")
    ep = lax.axis_index("ep")
    y, c = rep // C, lax.rem(rep, C)
    x, z = ep // Z, lax.rem(ep, Z)
    zhi, zlo = z // ZQ, lax.rem(z, ZQ)
    f32, bf16 = jnp.float32, jnp.bfloat16

    def wrap(v, n):
        return lax.rem(v + n, n)

    def at_rep(r):
        return {"rep": r, "ep": ep}

    def at_ep(e):
        return {"rep": rep, "ep": e}

    def at_z(d):
        return at_ep(x * Z + wrap(z + d, Z))

    xl, xri, xo = wrap(x - 1, X), wrap(x + 1, X), wrap(x + 2, X)
    yl, yri, yo = wrap(y - 1, Y), wrap(y + 1, Y), wrap(y + 2, Y)
    dev_x = (at_ep(xl * Z + z), at_ep(xri * Z + z))
    dev_y = (at_rep(yl * C + c), at_rep(yri * C + c))
    dev_sib = at_rep(y * C + 1 - c)
    rdev = [lax.rem(rep + d, REP) for d in range(1, REP)]

    pending = []

    def send(src, dst, dev):
        k = len(pending)
        copy = pltpu.make_async_remote_copy(
            src_ref=src, dst_ref=dst, send_sem=ssem.at[k], recv_sem=rsem.at[k], device_id=dev, device_id_type=MESH
        )
        copy.start()
        pending.append(copy)
        return copy

    def share(ref, dev):
        return send(ref, ref, dev)

    barrier = pltpu.get_barrier_semaphore()
    def at_class(k, r):
        return {"rep": r, "ep": x * Z + wrap(zhi + k, ZQ) * ZQ + zlo}

    spread = [(k, at_class(k, lax.rem(rep + d, REP)), d) for k in range(ZQ) for d in range(REP) if k or d]
    def at_xz(xx, d):
        return at_ep(xx * Z + wrap(z + d, Z))

    partners = [dev for _, dev, _ in spread]
    partners += [at_xz(xx, d) for xx in (xl, xri, xo) for d in (0, 1, -1, 2, -2)]
    partners += [at_z(d) for d in (1, -1, 2, -2)]
    for dev in partners:
        pl.semaphore_signal(barrier, inc=1, device_id=dev, device_id_type=MESH)
    loads = [
        pltpu.make_async_copy(gw.at[0], W.at[:, 0:HID], lsem.at[0]),
        pltpu.make_async_copy(uw.at[0], W.at[:, HID:2 * HID], lsem.at[1]),
    ]
    for load in loads:
        load.start()

    values = hid[...].astype(f32)
    inverse_rms = lax.rsqrt(jnp.mean(values * values, axis=-1, keepdims=True) + epsilon)
    normed = (values * inverse_rms * gain[...]).astype(bf16)
    for r in range(REP):
        SA[r] = normed[:, r * SLICE:(r + 1) * SLICE]
    exp_logits = jnp.exp(logits[...])
    probs = exp_logits / jnp.sum(exp_logits, axis=0, keepdims=True)
    high = probs.astype(bf16).astype(f32)
    middle = (probs - high).astype(bf16).astype(f32)
    stacked = jnp.concatenate([ids[...].astype(f32), high, middle, probs - high - middle], axis=0)
    shape = (4 * TOP, 128)
    pick = lax.broadcasted_iota(jnp.int32, shape, 0) == lax.broadcasted_iota(jnp.int32, shape, 1)
    T[x, zhi, zlo] = lax.dot_general(
        stacked.astype(bf16), pick.astype(f32).astype(bf16), (((0,), (0,)), ((), ())), preferred_element_type=f32
    ).astype(bf16)
    pl.semaphore_wait(barrier, len(partners))

    first = [send(SA.at[lax.rem(rep + d, REP)], SB.at[zhi, rep], dev) for _, dev, d in spread]
    tlevel = [share(T.at[x, zhi, zlo], at_class(k, rep)) for k in range(1, ZQ)]
    def down_slice(r):
        return dw.at[0, :, pl.ds(pl.multiple_of(r * SLICE, SLICE), SLICE)]

    distant = [yy * C + cc for yy in (yo, yri, yl) for cc in (c, 1 - c)] + [y * C + 1 - c]
    downs = [send(down_slice(r), DT.at[rep], at_rep(r)) for r in distant]
    own_down = pltpu.make_async_copy(down_slice(rep), DT.at[rep], lsem.at[2])
    own_down.start()
    SB[zhi, rep] = SA[rep]
    for copy in first:
        copy.wait_recv()
    q0 = rep * 2
    for k in range(ZQ):
        for r in range(REP):
            BF[k, 2 * r:2 * r + 2, :] = SB[k, r].astype(f32)
    for k in range(ZQ):
        block = BF[k].astype(bf16)
        R[q0, x, k, zlo] = block[:, :HALF]
        R[q0 + 1, x, k, zlo] = block[:, HALF:]
    both = R.at[pl.ds(q0, 2), x, :, zlo]
    level = [share(both, at_z(1)), share(both, at_z(-1))]
    level += [share(R.at[q0, x, :, zlo], at_z(2)), share(R.at[q0 + 1, x, :, zlo], at_z(-2))]
    for copy in tlevel:
        copy.wait_recv()
    tlevel = [share(T.at[x, :, zlo], at_z(d)) for d in (1, -1, 2)]

    class Ring:
        def __init__(self, view, me, n, devs):
            self.view, self.me, self.devs = view, me, devs
            self.lo, self.hi = wrap(me - 1, n), wrap(me + 1, n)

        def put(self, who, half, side):
            return share(self.view(who, half), self.devs[side])

        def first(self):
            self.ra = self.put(self.me, 0, 1)
            self.lb = self.put(self.me, 1, 0)
            self.rb = self.put(self.me, 1, 1)
            self.la = self.put(self.me, 0, 0)
            return self

        def relay(self):
            self.ra.wait_recv()
            self.oa = self.put(self.lo, 0, 1)
            self.lb.wait_recv()
            self.ob = self.put(self.hi, 1, 0)

        def low(self):
            self.rb.wait_recv()

        def high(self):
            self.la.wait_recv()

        def far(self):
            self.oa.wait_recv()
            self.ob.wait_recv()

    def piece(yy, h, xx):
        return R.at[(yy * C + c) * 2 + h, xx]

    def cut(ref, half):
        return ref.at[pl.ds(2 * half, 2)]

    def along_y(h, xx):
        return Ring(lambda s, half: cut(piece(s, h, xx), half), y, Y, dev_y)

    def along_x(h, yy):
        return Ring(lambda s, half: cut(piece(yy, h, s), half), x, X, dev_x)

    sib = {}

    def forward(yy, h, xx, name):
        sib[name + (h,)] = share(piece(yy, h, xx), dev_sib)

    for load in loads:
        load.wait()
    for copy in level:
        copy.wait_recv()
    x1 = along_x(0, y).first()
    y1 = along_y(1, x).first()
    y2 = {"own": along_y(0, x).first()}
    x2 = {"own": along_x(1, y).first()}
    forward(y, 0, x, ("own", "own"))
    forward(y, 1, x, ("own", "own"))
    x1.relay()
    y1.relay()
    x1.low()
    y2["low"] = along_y(0, xl).first()
    y1.low()
    x2["low"] = along_x(1, yl).first()
    x1.high()
    y2["high"] = along_y(0, xri).first()
    y1.high()
    x2["high"] = along_x(1, yri).first()
    forward(y, 0, xl, ("own", "low"))
    forward(y, 0, xri, ("own", "high"))
    forward(yl, 1, x, ("low", "own"))
    forward(yri, 1, x, ("high", "own"))
    y2["own"].relay()
    x2["own"].relay()
    x1.far()
    y2["far"] = along_y(0, xo).first()
    y1.far()
    x2["far"] = along_x(1, yo).first()
    forward(y, 0, xo, ("own", "far"))
    forward(yo, 1, x, ("far", "own"))
    xname = {"own": x, "low": xl, "high": xri, "far": xo}
    yname = {"own": y, "low": yl, "high": yri, "far": yo}

    def near_y(g):
        y2[g].low()
        forward(yl, 0, xname[g], ("low", g))
        y2[g].high()
        forward(yri, 0, xname[g], ("high", g))

    def far_y(g):
        y2[g].far()
        forward(yo, 0, xname[g], ("far", g))

    def near_x(g):
        x2[g].low()
        forward(yname[g], 1, xl, (g, "low"))
        x2[g].high()
        forward(yname[g], 1, xri, (g, "high"))

    def far_x(g):
        x2[g].far()
        forward(yname[g], 1, xo, (g, "far"))

    def gathered(g):
        for name in list(sib):
            if name[1] == g:
                sib.pop(name).wait_recv()

    def gateup(xx):
        total = None
        for q in range(2 * REP):
            part = jnp.dot(
                R[q, xx].reshape(XROWS, HALF), W[q * HALF:(q + 1) * HALF, :], preferred_element_type=f32
            )
            total = part if total is None else total + part
        ACC[...] = total
        for i in range(2):
            at = slice(i * 128, (i + 1) * 128)
            gate_part = ACC[at, 0:HID]
            up_part = ACC[at, HID:2 * HID]
            HF[y, c, xx, at, :] = (gate_part / (1.0 + jnp.exp(-gate_part)) * up_part).astype(bf16)

    hrings = {}
    hsibs = {}

    def hstart(g):
        xx = xname[g]
        hrings[g] = Ring(lambda s, half: HF.at[s, c, xx, pl.ds(half * 128, 128)], y, Y, dev_y).first()
        hsibs[g] = [share(HF.at[y, c, xx], dev_sib)]

    def hnear(g):
        xx = xname[g]
        hrings[g].relay()
        hrings[g].low()
        hsibs[g].append(share(HF.at[yl, c, xx], dev_sib))
        hrings[g].high()
        hsibs[g].append(share(HF.at[yri, c, xx], dev_sib))

    def hfar(g):
        hrings[g].far()
        hsibs[g].append(share(HF.at[yo, c, xname[g]], dev_sib))

    def hdone(g):
        for copy in hsibs[g]:
            copy.wait_recv()

    for copy in tlevel:
        copy.wait_recv()
    ring_t = Ring(lambda s, h: T.at[s, pl.ds(2 * h, 2)], x, X, dev_x).first()
    near_y("own")
    near_x("own")
    y2["low"].relay()
    x2["low"].relay()
    y2["high"].relay()
    x2["high"].relay()
    far_y("own")
    far_x("own")
    gathered("own")
    gateup(x)
    hstart("own")
    near_y("low")
    near_x("low")
    near_y("high")
    near_x("high")
    y2["far"].relay()
    x2["far"].relay()
    far_y("low")
    far_x("low")
    far_y("high")
    far_x("high")
    hnear("own")
    near_y("far")
    near_x("far")
    gathered("low")
    gateup(xl)
    hstart("low")
    gathered("high")
    gateup(xri)
    hstart("high")
    far_y("far")
    far_x("far")
    ring_t.relay()
    hfar("own")
    hnear("low")
    hnear("high")
    gathered("far")
    gateup(xo)
    hlast = [share(HF.at[y, c, xo], at_rep(to * C + c)) for to in (yo, yl, yri)]
    hsibs["far"] = [share(HF.at[y, c, xo], dev_sib)]
    ring_t.low()
    ring_t.high()
    ring_t.far()
    own_down.wait()
    for copy in downs:
        copy.wait_recv()

    expert = ep.astype(f32)
    lane = lax.broadcasted_iota(jnp.int32, (XROWS, 128), 1)

    def project(xx):
        t = T[xx].reshape(XROWS, 128).astype(f32)
        parts = pltpu.roll(t, 128 - TOP, 1) + (pltpu.roll(t, 128 - 2 * TOP, 1) + pltpu.roll(t, 128 - 3 * TOP, 1))
        scale = jnp.sum(jnp.where((lane < TOP) & (t == expert), parts, 0.0), axis=1, keepdims=True)
        total = jnp.zeros((XROWS, SLICE), f32)
        for yy in range(Y):
            act = jnp.concatenate([HF[yy, 0, xx], HF[yy, 1, xx]], axis=1)
            down = DT[2 * yy:2 * yy + 2].reshape(2 * HID, SLICE)
            total += jnp.dot(act, down, preferred_element_type=f32)
        return total * scale

    def part(xx):
        total = project(xx).astype(bf16)
        for h in range(2):
            for zz in range(Z):
                PB[xx, h, zz % ZQ, zz // ZQ] = total[zz * COL:(zz + 1) * COL, h * HALF:(h + 1) * HALF]

    scattered = []

    def scatter(xx, own):
        if own:
            ZA[x, 0] = PB[x, :, zlo]
        else:
            scattered.append(send(PB.at[xx, :, zlo], ZA.at[x, 0], at_xz(xx, 0)))
        for k, d in ((1, 1), (2, -1)):
            scattered.append(send(PB.at[xx, :, wrap(zlo + d, ZQ)], ZA.at[x, k], at_xz(xx, d)))
        for k, d in ((0, 2), (1, -2)):
            scattered.append(send(PB.at[xx, k, wrap(zlo + 2, ZQ)], ZB.at[x, k], at_xz(xx, d)))

    hfar("low")
    hfar("high")
    hdone("low")
    part(xl)
    scatter(xl, False)
    hdone("high")
    part(xri)
    scatter(xri, False)
    hdone("own")
    part(x)
    scatter(x, True)
    for copy, who in zip(hlast[1:] + hlast[:1], (yri, yl, yo)):
        copy.wait_recv()
        hsibs["far"].append(share(HF.at[who, c, xo], dev_sib))
    hdone("far")
    part(xo)
    scatter(xo, False)
    for copy in scattered:
        copy.wait_recv()
    for h in range(2):
        total = jnp.zeros((ZQ, COL, HALF), f32)
        for xx in range(X):
            for k in range(3):
                total += ZA[xx, k, h].astype(f32)
            total += ZB[xx, h].astype(f32)
        for k in range(ZQ):
            BF[k, :, h * HALF:(h + 1) * HALF] = total[k]
    for k in range(ZQ):
        for r in range(REP):
            FA[k, r] = BF[k, 2 * r:2 * r + 2, :].astype(bf16)
    last = [
        send(FA.at[wrap(zhi + k, ZQ), lax.rem(rep + d, REP)], FB.at[zhi, rep], dev) for k, dev, d in spread
    ]
    FB[zhi, rep] = FA[zhi, rep]
    for copy in pending[:-len(last)]:
        copy.wait_send()
    for copy in last:
        copy.wait_recv()
    for r in range(REP):
        total = FB[0, r].astype(f32)
        for k in range(1, ZQ):
            total += FB[k, r].astype(f32)
        out[:, r * SLICE:(r + 1) * SLICE] = total.astype(bf16)
    for copy in last:
        copy.wait_send()


def on_device(
    hidden_state, norm_gain, expert_ids, gate_logits, gate_weight, up_weight, down_weight
):
    bf, f32 = jnp.bfloat16, jnp.float32
    vmem = pl.BlockSpec(memory_space=pltpu.VMEM)
    hbm = pl.BlockSpec(memory_space=pl.ANY)
    dma = pltpu.SemaphoreType.DMA
    return pl.pallas_call(
        kernel,
        out_shape=jax.ShapeDtypeStruct((COL // REP, D), bf),
        in_specs=[vmem, vmem, vmem, vmem, hbm, hbm, hbm],
        out_specs=vmem,
        scratch_shapes=[
            pltpu.VMEM((REP, 2, SLICE), bf),
            pltpu.VMEM((ZQ, REP, 2, SLICE), bf),
            pltpu.VMEM((ZQ, COL, SLICE), f32),
            pltpu.VMEM((2 * REP, X, ZQ, ZQ, COL, HALF), bf),
            pltpu.VMEM((X, ZQ, ZQ, COL, 128), bf),
            pltpu.VMEM((D, 2 * HID), bf),
            pltpu.VMEM((XROWS, 2 * HID), f32),
            pltpu.VMEM((Y, C, X, XROWS, HID), bf),
            pltpu.VMEM((REP, HID, SLICE), bf),
            pltpu.VMEM((X, 2, ZQ, ZQ, COL, HALF), bf),
            pltpu.VMEM((X, 3, 2, ZQ, COL, HALF), bf),
            pltpu.VMEM((X, 2, ZQ, COL, HALF), bf),
            pltpu.VMEM((ZQ, REP, 2, SLICE), bf),
            pltpu.VMEM((ZQ, REP, 2, SLICE), bf),
            dma((3,)),
            dma((SENDS,)),
            dma((SENDS,)),
        ],
        compiler_params=pltpu.CompilerParams(
            collective_id=0, has_side_effects=True, vmem_limit_bytes=56 * 1024 * 1024
        ),
    )(hidden_state, norm_gain.reshape(1, D), expert_ids.T, gate_logits.T, gate_weight, up_weight, down_weight)


def solution(mesh):
    placed = (
        P(("ep", "rep"), None),
        P(),
        P("ep", None),
        P("ep", None),
        P("ep", None, "rep"),
        P("ep", None, "rep"),
        P("ep", "rep", None),
    )
    return jax.shard_map(
        on_device, mesh=mesh, in_specs=placed, out_specs=P(("ep", "rep"), None), check_vma=False
    )
```
